128 devices in a mesh: dp: 8 (over y, z_hi), mp: 16 (over z_lo, x, core).
Axes of the slice: x: 4, y: 4, z: 4 (z_hi: 2, z_lo: 2; z = z_hi * 2 + z_lo), core: 2. Of those that a mesh axis runs over, the one named last changes fastest.
Arguments:
- grad: bfloat16 [8192, 16384], P(('dp', 'mp')), as said below
- block_owner: int32 [128], replicated, may hold values from 0 to 127, as said below
- left_stat: float32 [128, 1024, 1024], P(('dp', 'mp')), as said below
- right_stat: float32 [128, 1024, 1024], P(('dp', 'mp')), as said below
- left_root: bfloat16 [128, 1024, 1024], P(('dp', 'mp'))
- right_root: bfloat16 [128, 1024, 1024], P(('dp', 'mp'))
Outputs:
- new_left: float32 [128, 1024, 1024], P(('dp', 'mp'))
- new_right: float32 [128, 1024, 1024], P(('dp', 'mp'))
- update: bfloat16 [8192, 16384], P(('dp', 'mp'))
The draws below stay inside these ranges and needn't reach their ends.
Inputs may be any that keep to these rules, and one draw needn't show every extreme that they name: `block_owner`: A permutation: each device owns exactly one block, and of each band's 16 blocks exactly 2 are owned by devices of each dp index (owner = dp index * 16 + mp index). `grad`: gradient entries, scaled per row and per column. `left_stat`: symmetric positive definite. `right_stat`: symmetric positive definite.
All inputs are finite; a program needn't handle non-finite values.
Results may differ from the reference program's by a relative error of at most 0.0039.
The reference program's roundings to bfloat16 on the way count: a program that leaves them out, or rounds other values in their place, can miss the bound.
Values may be sent and summed in bfloat16 or wider, within the bound.
A program may use at most 256 MiB of HBM per device.

```python
import jax
import jax.numpy as jnp
from jax import lax

BLK = 1024
BANDS = 8
COLB = 16
GROUP = 2
NB = 128
ROWS = 8192
COLS = 16384


def draw_grad(key, part):
    key_base, key_rows, key_cols = jax.random.split(jax.random.fold_in(key, 11), 3)
    ramp = 10.0 ** (jnp.arange(ROWS, dtype=jnp.float32) / ROWS)
    row_factor = jnp.exp(jax.random.uniform(key_rows, (ROWS, 1), jnp.float32) * jnp.log(3.0))
    base = jax.random.normal(key_base, (ROWS, COLS), jnp.float32)
    col_factor = jnp.exp(jax.random.uniform(key_cols, (1, COLS), jnp.float32) * jnp.log(3.0))
    return (base * ramp[:, None] * row_factor * col_factor).astype(jnp.bfloat16)


def root_matrix(key):
    key_diag, key_off = jax.random.split(key)
    diagonal = jnp.exp(jax.random.uniform(key_diag, (NB, BLK), jnp.float32, jnp.log(0.5), jnp.log(2.0)))
    off_part = jax.random.normal(key_off, (NB, BLK, BLK), jnp.float32)
    eye = jnp.eye(BLK, dtype=jnp.float32)
    return (eye[None] * diagonal[:, :, None] + off_part * (0.5 / BLK ** 0.5)).astype(jnp.bfloat16)


def stat_block(key):
    key_mat, key_level = jax.random.split(key)
    factor_mat = jax.random.normal(key_mat, (BLK, BLK), jnp.float32)
    level = jnp.exp(jax.random.uniform(key_level, (), jnp.float32, jnp.log(0.02), jnp.log(0.3)))
    gram = jnp.dot(factor_mat, factor_mat.T, precision=lax.Precision.HIGHEST) / BLK
    return level * (gram + 0.25 * jnp.eye(BLK, dtype=jnp.float32))


def stat_matrix(key):
    return lax.map(stat_block, jax.random.split(key, NB))


def draw_left_stat(key, part):
    return stat_matrix(jax.random.fold_in(key, 41))


def draw_right_stat(key, part):
    return stat_matrix(jax.random.fold_in(key, 42))


def draw_left_root(key, part):
    return root_matrix(jax.random.fold_in(key, 21))


def draw_right_root(key, part):
    return root_matrix(jax.random.fold_in(key, 22))


def draw_block_owner(key, part):
    key_cols, key_mps = jax.random.split(jax.random.fold_in(key, 31))
    col_perm = jax.vmap(lambda k: jax.random.permutation(k, COLB))(jax.random.split(key_cols, BANDS)).astype(jnp.int32)
    mp_perm = jax.vmap(lambda k: jax.random.permutation(k, COLB))(jax.random.split(key_mps, BANDS)).astype(jnp.int32)
    ranks = jnp.arange(COLB, dtype=jnp.int32)[None, :]
    band_ids = jnp.arange(BANDS, dtype=jnp.int32)[:, None]
    dp_target = ranks // GROUP
    item_index = band_ids * GROUP + ranks % GROUP
    owners = dp_target * COLB + mp_perm[dp_target, item_index]
    flat_index = (band_ids * COLB + col_perm).reshape(-1)
    return jnp.zeros((NB,), jnp.int32).at[flat_index].set(owners.reshape(-1).astype(jnp.int32))


def setup_inputs(seed: int = 0) -> dict:
    seeds = jax.random.split(jax.random.key(seed), 7)
    grad = draw_grad(jax.random.fold_in(seeds[6], 71), 0)
    block_owner = draw_block_owner(jax.random.fold_in(seeds[6], 71), 0)
    left_stat = draw_left_stat(jax.random.fold_in(seeds[6], 71), 0)
    right_stat = draw_right_stat(jax.random.fold_in(seeds[6], 71), 0)
    left_root = draw_left_root(jax.random.fold_in(seeds[6], 71), 0)
    right_root = draw_right_root(jax.random.fold_in(seeds[6], 71), 0)
    return dict(grad=grad, block_owner=block_owner, left_stat=left_stat, right_stat=right_stat, left_root=left_root, right_root=right_root)


clip_level = 0.5
beta_stat = 0.95

def owner_step(items, scale):
    block, left_old, right_old, left_inv, right_inv = items
    left_gram = jnp.dot(block, block.T, preferred_element_type=jnp.float32)
    right_gram = jnp.dot(block.T, block, preferred_element_type=jnp.float32)
    factor = (1.0 - beta_stat) * scale * scale / BLK
    left_new = beta_stat * left_old + factor * left_gram
    right_new = beta_stat * right_old + factor * right_gram
    partial_left = jnp.dot(left_inv, block, preferred_element_type=jnp.float32).astype(jnp.bfloat16)
    update_block = (jnp.dot(partial_left, right_inv, preferred_element_type=jnp.float32) * scale).astype(jnp.bfloat16)
    return (left_new, right_new, update_block)

def reference(grad, block_owner, left_stat, right_stat, left_root, right_root):
    values = grad.astype(jnp.float32)
    mean_square = jnp.sum(values * values) / (ROWS * COLS)
    scale = clip_level / jnp.sqrt(mean_square + 1e-06)
    blocks = grad.reshape(BANDS, BLK, COLB, BLK).transpose(0, 2, 1, 3).reshape(NB, BLK, BLK)
    block_of = jnp.argsort(block_owner).astype(jnp.int32)
    owned = jnp.take(blocks, block_of, axis=0)
    new_left, new_right, updates = lax.map(lambda items: owner_step(items, scale), (owned, left_stat, right_stat, left_root, right_root))
    back = jnp.take(updates, block_owner.astype(jnp.int32), axis=0)
    update = back.reshape(BANDS, COLB, BLK, BLK).transpose(0, 2, 1, 3).reshape(ROWS, COLS)
    return (new_left, new_right, update)
```

```python
import functools

import jax
import jax.numpy as jnp
from jax import lax
from jax.experimental import pallas as pl
from jax.experimental.pallas import tpu as pltpu
from jax.sharding import PartitionSpec as P

MESH = pl.DeviceIdType.MESH
BLK = 1024
DPN = 8
MPN = 16
SHARD = 64
ROWT = 16
KR = SHARD // ROWT
KC = 2
K = KR * KC
WID = BLK // KC
AHEAD = 3
BEHIND = 2
TILE = 256

clip_level = 0.5
beta_stat = 0.95


def xor(value, mask):
    bit = 1
    while bit <= mask:
        if mask & bit:
            value = value + bit * (1 - 2 * ((value // bit) % 2))
        bit *= 2
    return value


def kernel(
    tab, grad, left, right, lroot, rroot, new_left, new_right, update, *scratch
):
    it = iter(scratch)
    gb = [next(it) for _ in range(KR)]
    s1 = next(it)
    r1 = [next(it) for _ in range(K)]
    s2 = next(it)
    gq = next(it)
    s3 = next(it)
    r3 = [next(it) for _ in range(K)]
    s4 = next(it)
    r5 = [next(it) for _ in range(K)]
    ob = next(it)
    lb, rb, la, pb = next(it), next(it), next(it), next(it)
    lst, rst = next(it), next(it)
    sq_own, sq_in1, sq_mid, sq_in2 = next(it), next(it), next(it), next(it)
    ssem, rsem, qs, qr, gsem, wsem, osem, tsem = (next(it) for _ in range(8))

    dp = lax.axis_index("dp")
    mp = lax.axis_index("mp")
    dp_peer = [(xor(dp, i), xor(mp, 8 * (i % 2))) for i in range(DPN)]
    mp_peer = [(dp, xor(mp, q)) for q in range(MPN)]

    barrier = pltpu.get_barrier_semaphore()
    for peer in dp_peer[1:] + mp_peer[1:]:
        pl.semaphore_signal(barrier, inc=1, device_id=peer, device_id_type=MESH)

    for r in range(KR):
        for n in range(MPN):
            here = (pl.ds(ROWT * r, ROWT), pl.ds(BLK * n, BLK))
            pltpu.make_async_copy(grad.at[here], gb[r].at[n], gsem.at[r]).start()

    def send(src, dst, phase, k, peer):
        pltpu.make_async_remote_copy(
            src_ref=src,
            dst_ref=dst,
            send_sem=ssem.at[phase, k],
            recv_sem=rsem.at[phase, k],
            device_id=peer,
            device_id_type=MESH,
        ).start()

    def take_bytes(ref, sem):
        pltpu.make_async_copy(ref, ref, sem).wait()

    seen = set()

    def first_hop(k):
        r, c = k // KC, k % KC
        if r not in seen:
            seen.add(r)
            take_bytes(gb[r], gsem.at[r])
        for i in list(range(1, DPN)) + [0]:
            for n in (2 * i, 2 * i + 1):
                piece = gb[r][tab[n], :, pl.ds(c * WID, WID)]
                if i:
                    s1[k, n] = piece
                else:
                    r1[k][n] = piece
            if i:
                if k == 0 and i == 1:
                    pl.semaphore_wait(barrier, DPN - 1 + MPN - 1)
                pair = pl.ds(2 * i, 2)
                send(s1.at[k, pair], r1[k].at[pair], 0, k, dp_peer[i])

    half, low = mp // 8, mp % 8

    def second_hop(k):
        r, c = k // KC, k % KC
        take_bytes(s1.at[k, pl.ds(2, MPN - 2)], rsem.at[0, k])
        for q in list(range(1, MPN)) + [0]:
            piece = r1[k][tab[16 + q]]
            here = gq.at[half, low, r, :, pl.ds(c * WID, WID)]
            if q:
                s2[k, q] = piece
                send(s2.at[k, q], here, 1, k, mp_peer[q])
            else:
                gq[half, low, r, :, pl.ds(c * WID, WID)] = piece

    def square_tile(r, acc):
        def body(n, acc):
            x = gb[r][n].astype(jnp.float32)
            x = x * x
            for w in range(BLK // 128):
                acc = acc + x[:8, w * 128 : (w + 1) * 128] + x[8:, w * 128 : (w + 1) * 128]
            return acc

        return lax.fori_loop(0, MPN, body, acc)

    def send_square(src, dst, stage, peer):
        pltpu.make_async_remote_copy(
            src_ref=src,
            dst_ref=dst,
            send_sem=qs.at[stage],
            recv_sem=qr.at[stage],
            device_id=peer,
            device_id_type=MESH,
        ).start()

    for k in range(min(AHEAD, K)):
        first_hop(k)
    for r in range(KR):
        if r not in seen:
            seen.add(r)
            take_bytes(gb[r], gsem.at[r])
    loads = [
        pltpu.make_async_copy(lroot, lb, wsem.at[0]),
        pltpu.make_async_copy(rroot, rb, wsem.at[1]),
        pltpu.make_async_copy(left, lst, wsem.at[2]),
        pltpu.make_async_copy(right, rst, wsem.at[3]),
    ]
    for c in loads:
        c.start()
    acc = jnp.zeros((8, 128), jnp.float32)
    for r in range(KR):
        acc = square_tile(r, acc)
    sq_own[...] = acc
    for i in range(1, DPN):
        send_square(sq_own, sq_in1.at[i], 0, dp_peer[i])
    for k in range(K):
        second_hop(k)
        if k + AHEAD < K:
            first_hop(k + AHEAD)
        if k == 1:
            take_bytes(sq_in1.at[pl.ds(1, DPN - 1)], qr.at[0])
            mid = sq_own[...]
            for i in range(1, DPN):
                mid = mid + sq_in1[i]
            sq_mid[...] = mid
            for q in range(1, MPN):
                send_square(sq_mid, sq_in2.at[q], 1, mp_peer[q])
    for c in loads:
        c.wait()
    take_bytes(sq_in2.at[pl.ds(1, MPN - 1)], qr.at[1])
    total = sq_mid[...]
    for q in range(1, MPN):
        total = total + sq_in2[q]
    total = jnp.sum(jnp.sum(total, axis=0, keepdims=True), axis=1, keepdims=True)
    mean_square = total / (DPN * BLK * MPN * BLK)
    scale = clip_level / jnp.sqrt(mean_square + 1e-06)
    factor = (1.0 - beta_stat) * scale * scale / BLK
    for k in range(K):
        take_bytes(s2.at[k, pl.ds(1, MPN - 1)], rsem.at[1, k])

    side = [tab[64], tab[65]]
    rows = MPN * ROWT

    def third_hop(k):
        r, c = k // KC, k % KC
        if c == 0:
            for h in range(2):
                la[pl.ds(h * rows // 2, rows // 2), :] = lb[side[h], :, r].reshape(
                    rows // 2, BLK
                )

            @pl.loop(0, BLK // TILE)
            def _(n):
                at = pl.ds(pl.multiple_of(n * TILE, TILE), TILE)
                out = jnp.dot(
                    la[:, : BLK // 2],
                    gq[side[0], :, :, :, at].reshape(BLK // 2, TILE),
                    preferred_element_type=jnp.float32,
                )
                out += jnp.dot(
                    la[:, BLK // 2 :],
                    gq[side[1], :, :, :, at].reshape(BLK // 2, TILE),
                    preferred_element_type=jnp.float32,
                )
                pb[:, at] = out.astype(jnp.bfloat16)

        for n in range(WID // TILE):
            out = jnp.dot(
                pb[...],
                rb[:, pl.ds(c * WID + n * TILE, TILE)],
                preferred_element_type=jnp.float32,
            )
            out = (out * scale).astype(jnp.bfloat16)
            s3[k, :, :, pl.ds(n * TILE, TILE)] = out.reshape(MPN, ROWT, TILE)
        for q in range(1, MPN):
            send(s3.at[k, mp_peer[q][1]], r3[k].at[q], 2, k, mp_peer[q])
        r3[k][0] = s3[k, mp]

    def fourth_hop(k):
        take_bytes(s2.at[k, pl.ds(1, MPN - 1)], rsem.at[2, k])
        for i in list(range(1, DPN)) + [0]:
            for n in (2 * i, 2 * i + 1):
                piece = r3[k][tab[32 + n]]
                if i:
                    s4[k, n] = piece
                else:
                    r5[k][n] = piece
            if i:
                pair = pl.ds(2 * i, 2)
                send(s4.at[k, pair], r5[k].at[pair], 3, k, dp_peer[i])

    stats_out = []

    def left_part(n):
        here = pl.ds(n * TILE, TILE)
        tiles = TILE // SHARD
        lhs = gq[side[n // 2], pl.ds((n % 2) * tiles, tiles)].reshape(TILE, BLK)
        for g in range(2):
            cols = pl.ds(g * BLK // 2, BLK // 2)
            gram = lax.dot_general(
                lhs,
                gq[side[g]].reshape(BLK // 2, BLK),
                (((1,), (1,)), ((), ())),
                preferred_element_type=jnp.float32,
            )
            lst[here, cols] = beta_stat * lst[here, cols] + factor * gram
        c = pltpu.make_async_copy(lst.at[here], new_left.at[here], tsem.at[n])
        c.start()
        stats_out.append(c)

    def right_part(n):
        here = pl.ds(n * TILE, TILE)
        gram = lax.dot_general(
            gq[:, :, :, :, here].reshape(BLK, TILE),
            gq[...].reshape(BLK, BLK),
            (((0,), (0,)), ((), ())),
            preferred_element_type=jnp.float32,
        )
        rst[here, :] = beta_stat * rst[here, :] + factor * gram
        c = pltpu.make_async_copy(rst.at[here], new_right.at[here], tsem.at[4 + n])
        c.start()
        stats_out.append(c)

    parts = [functools.partial(left_part, n) for n in range(4)]
    parts += [functools.partial(right_part, n) for n in range(4)]

    for k in range(K + BEHIND):
        if k < K:
            third_hop(k)
        if k >= BEHIND:
            fourth_hop(k - BEHIND)
            if parts:
                parts.pop(0)()
    for part in parts:
        part()

    update_out = []
    for k in range(K):
        r, c = k // KC, k % KC
        take_bytes(s1.at[k, pl.ds(2, MPN - 2)], rsem.at[3, k])
        for col in range(MPN):
            here = pl.ds(col * BLK + c * WID, WID)
            ob[pl.ds(r * ROWT, ROWT), here] = r5[k][tab[48 + col]]
        if c == KC - 1:
            here = pl.ds(r * ROWT, ROWT)
            cp = pltpu.make_async_copy(ob.at[here], update.at[here], osem.at[r])
            cp.start()
            update_out.append(cp)

    for k in range(K):
        take_bytes(s1.at[k, pl.ds(2, MPN - 2)], ssem.at[0, k])
        take_bytes(s2.at[k, pl.ds(1, MPN - 1)], ssem.at[1, k])
        take_bytes(s2.at[k, pl.ds(1, MPN - 1)], ssem.at[2, k])
        take_bytes(s1.at[k, pl.ds(2, MPN - 2)], ssem.at[3, k])
    take_bytes(sq_in1.at[pl.ds(1, DPN - 1)], qs.at[0])
    take_bytes(sq_in2.at[pl.ds(1, MPN - 1)], qs.at[1])
    for cp in stats_out + update_out:
        cp.wait()


def tables(block_owner, dp, mp):
    owner = block_owner.reshape(DPN, MPN)
    rank = jnp.sum((owner[:, None, :] < owner[:, :, None]).astype(jnp.int32), axis=2)
    sixteen = jnp.arange(MPN, dtype=jnp.int32)
    mine = lax.dynamic_index_in_dim(rank, dp, 0, keepdims=False)
    col_slot = ((mine // 2) ^ dp) * 2 + mine % 2
    slot_col = jnp.sum(
        jnp.where(col_slot[None, :] == sixteen[:, None], sixteen[None, :], 0), axis=1
    )
    bands = jnp.arange(DPN, dtype=jnp.int32)
    slot = ((bands ^ dp) * 2)[:, None] + rank % 2
    want = dp * MPN + (mp ^ sixteen)
    hop_slot = jnp.sum(
        jnp.where(owner[None] == want[:, None, None], slot[None], 0), axis=(1, 2)
    )
    slot_hop = jnp.sum(
        jnp.where(hop_slot[None, :] == sixteen[:, None], sixteen[None, :], 0), axis=1
    )
    flipped = (hop_slot[:1] // 2) % 2
    return jnp.concatenate(
        [slot_col, hop_slot, slot_hop, col_slot, flipped, 1 - flipped]
    )


def per_device(grad, block_owner, left_stat, right_stat, left_root, right_root):
    dp = lax.axis_index("dp")
    mp = lax.axis_index("mp")
    tab = tables(block_owner, dp, mp)
    bf, f32 = jnp.bfloat16, jnp.float32
    hbm = pl.BlockSpec(memory_space=pl.ANY)
    hop = (MPN, ROWT, WID)
    dma = pltpu.SemaphoreType.DMA
    new_left, new_right, update = pl.pallas_call(
        kernel,
        name="shampoo",
        out_shape=(
            jax.ShapeDtypeStruct((BLK, BLK), f32),
            jax.ShapeDtypeStruct((BLK, BLK), f32),
            jax.ShapeDtypeStruct(grad.shape, bf),
        ),
        in_specs=[pl.BlockSpec(memory_space=pltpu.SMEM)]
        + [pl.BlockSpec(memory_space=pltpu.HBM)] * 5,
        out_specs=(hbm, hbm, hbm),
        scratch_shapes=[pltpu.VMEM((MPN, ROWT, BLK), bf) for _ in range(KR)]
        + [pltpu.VMEM((K, *hop), bf)]
        + [pltpu.VMEM(hop, bf) for _ in range(K)]
        + [pltpu.VMEM((K, *hop), bf)]
        + [pltpu.VMEM((2, 8, KR, ROWT, BLK), bf)]
        + [pltpu.VMEM((K, *hop), bf)]
        + [pltpu.VMEM(hop, bf) for _ in range(K)]
        + [pltpu.VMEM((K, *hop), bf)]
        + [pltpu.VMEM(hop, bf) for _ in range(K)]
        + [pltpu.VMEM((SHARD, MPN * BLK), bf)]
        + [
            pltpu.VMEM((2, 8, KR, ROWT, BLK), bf),
            pltpu.VMEM((BLK, BLK), bf),
            pltpu.VMEM((MPN * ROWT, BLK), bf),
            pltpu.VMEM((MPN * ROWT, BLK), bf),
            pltpu.VMEM((BLK, BLK), f32),
            pltpu.VMEM((BLK, BLK), f32),
            pltpu.VMEM((8, 128), f32),
            pltpu.VMEM((DPN, 8, 128), f32),
            pltpu.VMEM((8, 128), f32),
            pltpu.VMEM((MPN, 8, 128), f32),
            dma((4, K)),
            dma((4, K)),
            dma((2,)),
            dma((2,)),
            dma((KR,)),
            dma((4,)),
            dma((KR,)),
            dma((8,)),
        ],
        compiler_params=pltpu.CompilerParams(
            collective_id=0, has_side_effects=True, vmem_limit_bytes=48 << 20
        ),
    )(
        tab,
        grad,
        left_stat[0],
        right_stat[0],
        left_root[0].reshape(2, 8, KR, ROWT, BLK),
        right_root[0],
    )
    return (new_left[None], new_right[None], update)


def solution(mesh):
    both = ("dp", "mp")
    in_specs = (
        P(both, None),
        P(),
        P(both, None, None),
        P(both, None, None),
        P(both, None, None),
        P(both, None, None),
    )
    out_specs = (P(both, None, None), P(both, None, None), P(both, None))
    return jax.shard_map(
        per_device, mesh=mesh, in_specs=in_specs, out_specs=out_specs, check_vma=False
    )
```

```python
import functools

import jax
import jax.numpy as jnp
from jax import lax
from jax.experimental import pallas as pl
from jax.experimental.pallas import tpu as pltpu
from jax.sharding import PartitionSpec as P

MESH = pl.DeviceIdType.MESH
BLK = 1024
DPN = 8
MPN = 16
SHARD = 64
ROWT = 16
KR = SHARD // ROWT
KC = 2
K = KR * KC
WID = BLK // KC
AHEAD = 3
BEHIND = 2
TILE = 256

clip_level = 0.5
beta_stat = 0.95


def xor(value, mask):
    bit = 1
    while bit <= mask:
        if mask & bit:
            value = value + bit * (1 - 2 * ((value // bit) % 2))
        bit *= 2
    return value


def kernel(
    tab, grad, left, right, lroot, rroot, lst, rst, ob, *scratch
):
    it = iter(scratch)
    gb = [next(it) for _ in range(KR)]
    s1 = next(it)
    r1 = [next(it) for _ in range(K)]
    s2 = next(it)
    gq = next(it)
    s3 = next(it)
    r3 = [next(it) for _ in range(K)]
    s4 = next(it)
    r5 = [next(it) for _ in range(K)]
    lb, rb, la, pb = next(it), next(it), next(it), next(it)
    sq_own, sq_in1, sq_mid, sq_in2 = next(it), next(it), next(it), next(it)
    ssem, rsem, qs, qr, gsem, wsem = (next(it) for _ in range(6))

    dp = lax.axis_index("dp")
    mp = lax.axis_index("mp")
    dp_peer = [(xor(dp, i), xor(mp, 8 * (i % 2))) for i in range(DPN)]
    mp_peer = [(dp, xor(mp, q)) for q in range(MPN)]

    barrier = pltpu.get_barrier_semaphore()
    for peer in dp_peer[1:] + mp_peer[1:]:
        pl.semaphore_signal(barrier, inc=1, device_id=peer, device_id_type=MESH)

    for r in range(KR):
        for n in range(MPN):
            here = (pl.ds(ROWT * r, ROWT), pl.ds(BLK * n, BLK))
            pltpu.make_async_copy(grad.at[here], gb[r].at[n], gsem.at[r]).start()

    def send(src, dst, phase, k, peer):
        pltpu.make_async_remote_copy(
            src_ref=src,
            dst_ref=dst,
            send_sem=ssem.at[phase, k],
            recv_sem=rsem.at[phase, k],
            device_id=peer,
            device_id_type=MESH,
        ).start()

    def take_bytes(ref, sem):
        pltpu.make_async_copy(ref, ref, sem).wait()

    seen = set()

    def first_hop(k):
        r, c = k // KC, k % KC
        if r not in seen:
            seen.add(r)
            take_bytes(gb[r], gsem.at[r])
        for i in list(range(1, DPN)) + [0]:
            for n in (2 * i, 2 * i + 1):
                piece = gb[r][tab[n], :, pl.ds(c * WID, WID)]
                if i:
                    s1[k, n] = piece
                else:
                    r1[k][n] = piece
            if i:
                if k == 0 and i == 1:
                    pl.semaphore_wait(barrier, DPN - 1 + MPN - 1)
                pair = pl.ds(2 * i, 2)
                send(s1.at[k, pair], r1[k].at[pair], 0, k, dp_peer[i])

    half, low = mp // 8, mp % 8

    def second_hop(k):
        r, c = k // KC, k % KC
        take_bytes(s1.at[k, pl.ds(2, MPN - 2)], rsem.at[0, k])
        for q in list(range(1, MPN)) + [0]:
            piece = r1[k][tab[16 + q]]
            here = gq.at[half, low, r, :, pl.ds(c * WID, WID)]
            if q:
                s2[k, q] = piece
                send(s2.at[k, q], here, 1, k, mp_peer[q])
            else:
                gq[half, low, r, :, pl.ds(c * WID, WID)] = piece

    def square_tile(r, acc):
        def body(n, acc):
            x = gb[r][n].astype(jnp.float32)
            x = x * x
            for w in range(BLK // 128):
                acc = acc + x[:8, w * 128 : (w + 1) * 128] + x[8:, w * 128 : (w + 1) * 128]
            return acc

        return lax.fori_loop(0, MPN, body, acc)

    def send_square(src, dst, stage, peer):
        pltpu.make_async_remote_copy(
            src_ref=src,
            dst_ref=dst,
            send_sem=qs.at[stage],
            recv_sem=qr.at[stage],
            device_id=peer,
            device_id_type=MESH,
        ).start()

    for k in range(min(AHEAD, K)):
        first_hop(k)
    for r in range(KR):
        if r not in seen:
            seen.add(r)
            take_bytes(gb[r], gsem.at[r])
    loads = [
        pltpu.make_async_copy(lroot, lb, wsem.at[0]),
        pltpu.make_async_copy(rroot, rb, wsem.at[1]),
        pltpu.make_async_copy(left, lst, wsem.at[2]),
        pltpu.make_async_copy(right, rst, wsem.at[3]),
    ]
    for c in loads:
        c.start()
    acc = jnp.zeros((8, 128), jnp.float32)
    for r in range(KR):
        acc = square_tile(r, acc)
    sq_own[...] = acc
    for i in range(1, DPN):
        send_square(sq_own, sq_in1.at[i], 0, dp_peer[i])
    for k in range(K):
        second_hop(k)
        if k + AHEAD < K:
            first_hop(k + AHEAD)
        if k == 1:
            take_bytes(sq_in1.at[pl.ds(1, DPN - 1)], qr.at[0])
            mid = sq_own[...]
            for i in range(1, DPN):
                mid = mid + sq_in1[i]
            sq_mid[...] = mid
            for q in range(1, MPN):
                send_square(sq_mid, sq_in2.at[q], 1, mp_peer[q])
    for c in loads:
        c.wait()
    take_bytes(sq_in2.at[pl.ds(1, MPN - 1)], qr.at[1])
    total = sq_mid[...]
    for q in range(1, MPN):
        total = total + sq_in2[q]
    total = jnp.sum(jnp.sum(total, axis=0, keepdims=True), axis=1, keepdims=True)
    mean_square = total / (DPN * BLK * MPN * BLK)
    scale = clip_level / jnp.sqrt(mean_square + 1e-06)
    factor = (1.0 - beta_stat) * scale * scale / BLK
    for k in range(K):
        take_bytes(s2.at[k, pl.ds(1, MPN - 1)], rsem.at[1, k])

    side = [tab[64], tab[65]]
    rows = MPN * ROWT

    def third_hop(k):
        r, c = k // KC, k % KC
        if c == 0:
            for h in range(2):
                la[pl.ds(h * rows // 2, rows // 2), :] = lb[side[h], :, r].reshape(
                    rows // 2, BLK
                )

            @pl.loop(0, BLK // TILE)
            def _(n):
                at = pl.ds(pl.multiple_of(n * TILE, TILE), TILE)
                out = jnp.dot(
                    la[:, : BLK // 2],
                    gq[side[0], :, :, :, at].reshape(BLK // 2, TILE),
                    preferred_element_type=jnp.float32,
                )
                out += jnp.dot(
                    la[:, BLK // 2 :],
                    gq[side[1], :, :, :, at].reshape(BLK // 2, TILE),
                    preferred_element_type=jnp.float32,
                )
                pb[:, at] = out.astype(jnp.bfloat16)

        for n in range(WID // TILE):
            out = jnp.dot(
                pb[...],
                rb[:, pl.ds(c * WID + n * TILE, TILE)],
                preferred_element_type=jnp.float32,
            )
            out = (out * scale).astype(jnp.bfloat16)
            s3[k, :, :, pl.ds(n * TILE, TILE)] = out.reshape(MPN, ROWT, TILE)
        for q in range(1, MPN):
            send(s3.at[k, mp_peer[q][1]], r3[k].at[q], 2, k, mp_peer[q])
        r3[k][0] = s3[k, mp]

    def fourth_hop(k):
        take_bytes(s2.at[k, pl.ds(1, MPN - 1)], rsem.at[2, k])
        for i in list(range(1, DPN)) + [0]:
            for n in (2 * i, 2 * i + 1):
                piece = r3[k][tab[32 + n]]
                if i:
                    s4[k, n] = piece
                else:
                    r5[k][n] = piece
            if i:
                pair = pl.ds(2 * i, 2)
                send(s4.at[k, pair], r5[k].at[pair], 3, k, dp_peer[i])

    def left_part(n):
        here = pl.ds(n * TILE, TILE)
        tiles = TILE // SHARD
        lhs = gq[side[n // 2], pl.ds((n % 2) * tiles, tiles)].reshape(TILE, BLK)
        for g in range(2):
            cols = pl.ds(g * BLK // 2, BLK // 2)
            gram = lax.dot_general(
                lhs,
                gq[side[g]].reshape(BLK // 2, BLK),
                (((1,), (1,)), ((), ())),
                preferred_element_type=jnp.float32,
            )
            lst[here, cols] = beta_stat * lst[here, cols] + factor * gram

    def right_part(n):
        here = pl.ds(n * TILE, TILE)
        gram = lax.dot_general(
            gq[:, :, :, :, here].reshape(BLK, TILE),
            gq[...].reshape(BLK, BLK),
            (((0,), (0,)), ((), ())),
            preferred_element_type=jnp.float32,
        )
        rst[here, :] = beta_stat * rst[here, :] + factor * gram

    parts = [functools.partial(left_part, n) for n in range(4)]
    parts += [functools.partial(right_part, n) for n in range(4)]

    for k in range(K + BEHIND):
        if k < K:
            third_hop(k)
        if k >= BEHIND:
            fourth_hop(k - BEHIND)
            if parts:
                parts.pop(0)()
    for part in parts:
        part()

    for k in range(K):
        r, c = k // KC, k % KC
        take_bytes(s1.at[k, pl.ds(2, MPN - 2)], rsem.at[3, k])
        for col in range(MPN):
            here = pl.ds(col * BLK + c * WID, WID)
            ob[pl.ds(r * ROWT, ROWT), here] = r5[k][tab[48 + col]]

    for k in range(K):
        take_bytes(s1.at[k, pl.ds(2, MPN - 2)], ssem.at[0, k])
        take_bytes(s2.at[k, pl.ds(1, MPN - 1)], ssem.at[1, k])
        take_bytes(s2.at[k, pl.ds(1, MPN - 1)], ssem.at[2, k])
        take_bytes(s1.at[k, pl.ds(2, MPN - 2)], ssem.at[3, k])
    take_bytes(sq_in1.at[pl.ds(1, DPN - 1)], qs.at[0])
    take_bytes(sq_in2.at[pl.ds(1, MPN - 1)], qs.at[1])


def move(*refs):
    count = (len(refs) - 1) // 2
    copies = [
        pltpu.make_async_copy(refs[n], refs[count + n], refs[-1].at[n])
        for n in range(count)
    ]
    for c in copies:
        c.start()
    for c in copies:
        c.wait()


def tables(owner, dp, mp):
    block = jnp.arange(DPN * MPN, dtype=jnp.int32)
    sixteen = jnp.arange(MPN, dtype=jnp.int32)
    band = block // MPN
    before = (band[:, None] == band[None, :]) & (owner[None, :] < owner[:, None])
    rank = jnp.sum(before.astype(jnp.int32), axis=1)
    mine = lax.dynamic_slice_in_dim(rank, dp * MPN, MPN)
    col_slot = ((mine >> 1) ^ dp) * 2 + (mine & 1)
    slot_col = jnp.sum(
        jnp.where(col_slot[None, :] == sixteen[:, None], sixteen[None, :], 0), axis=1
    )
    slot = (band ^ dp) * 2 + (rank & 1)
    want = dp * MPN + (mp ^ sixteen)
    hop_slot = jnp.sum(
        jnp.where(owner[None, :] == want[:, None], slot[None, :], 0), axis=1
    )
    slot_hop = jnp.sum(
        jnp.where(hop_slot[None, :] == sixteen[:, None], sixteen[None, :], 0), axis=1
    )
    flipped = (hop_slot[:1] >> 1) & 1
    return jnp.concatenate(
        [slot_col, hop_slot, slot_hop, col_slot, flipped, 1 - flipped]
    )


def per_device(grad, block_owner, left_stat, right_stat, left_root, right_root):
    dp = lax.axis_index("dp")
    mp = lax.axis_index("mp")
    tab = tables(block_owner, dp, mp)
    bf, f32 = jnp.bfloat16, jnp.float32
    hbm = pl.BlockSpec(memory_space=pl.ANY)
    hop = (MPN, ROWT, WID)
    dma = pltpu.SemaphoreType.DMA
    vmem = pl.BlockSpec(memory_space=pltpu.VMEM)
    outs = (((BLK, BLK), f32), ((BLK, BLK), f32), (grad.shape, bf))
    done = pl.pallas_call(
        kernel,
        name="shampoo",
        out_shape=tuple(pltpu.VMEM(*o) for o in outs),
        in_specs=[pl.BlockSpec(memory_space=pltpu.SMEM)]
        + [pl.BlockSpec(memory_space=pltpu.HBM)] * 5,
        out_specs=(vmem, vmem, vmem),
        scratch_shapes=[pltpu.VMEM((MPN, ROWT, BLK), bf) for _ in range(KR)]
        + [pltpu.VMEM((K, *hop), bf)]
        + [pltpu.VMEM(hop, bf) for _ in range(K)]
        + [pltpu.VMEM((K, *hop), bf)]
        + [pltpu.VMEM((2, 8, KR, ROWT, BLK), bf)]
        + [pltpu.VMEM((K, *hop), bf)]
        + [pltpu.VMEM(hop, bf) for _ in range(K)]
        + [pltpu.VMEM((K, *hop), bf)]
        + [pltpu.VMEM(hop, bf) for _ in range(K)]
        + [
            pltpu.VMEM((2, 8, KR, ROWT, BLK), bf),
            pltpu.VMEM((BLK, BLK), bf),
            pltpu.VMEM((MPN * ROWT, BLK), bf),
            pltpu.VMEM((MPN * ROWT, BLK), bf),
            pltpu.VMEM((8, 128), f32),
            pltpu.VMEM((DPN, 8, 128), f32),
            pltpu.VMEM((8, 128), f32),
            pltpu.VMEM((MPN, 8, 128), f32),
            dma((4, K)),
            dma((4, K)),
            dma((2,)),
            dma((2,)),
            dma((KR,)),
            dma((4,)),
        ],
        compiler_params=pltpu.CompilerParams(
            collective_id=0, has_side_effects=True, vmem_limit_bytes=44 << 20
        ),
    )(
        tab,
        grad,
        left_stat[0],
        right_stat[0],
        left_root[0].reshape(2, 8, KR, ROWT, BLK),
        right_root[0],
    )
    new_left, new_right, update = pl.pallas_call(
        move,
        name="move",
        out_shape=tuple(jax.ShapeDtypeStruct(*o) for o in outs),
        in_specs=(vmem,) * 3,
        out_specs=(hbm,) * 3,
        scratch_shapes=[dma((3,))],
        compiler_params=pltpu.CompilerParams(vmem_limit_bytes=1 << 20),
    )(*(pltpu.with_memory_space_constraint(d, pltpu.VMEM) for d in done))
    return (new_left[None], new_right[None], update)


def solution(mesh):
    both = ("dp", "mp")
    in_specs = (
        P(both, None),
        P(),
        P(both, None, None),
        P(both, None, None),
        P(both, None, None),
        P(both, None, None),
    )
    out_specs = (P(both, None, None), P(both, None, None), P(both, None))
    return jax.shard_map(
        per_device, mesh=mesh, in_specs=in_specs, out_specs=out_specs, check_vma=False
    )
```

```python
import functools

import jax
import jax.numpy as jnp
from jax import lax
from jax.experimental import pallas as pl
from jax.experimental.pallas import tpu as pltpu
from jax.sharding import PartitionSpec as P

MESH = pl.DeviceIdType.MESH
BLK = 1024
DPN = 8
MPN = 16
SHARD = 64
ROWT = 16
KR = SHARD // ROWT
CHUNKS = [(row, col, 512) for row in range(4) for col in (0, 512)]
K = len(CHUNKS)
AHEAD = 3
BEHIND = 2
TILE = 256
MOVES = 4

clip_level = 0.5
beta_stat = 0.95


def steps(value, bits):
    return [
        (1 << bit) * (1 - 2 * lax.rem(lax.div(value, 1 << bit), 2)) for bit in range(bits)
    ]


def xor(value, mask, step):
    for bit, amount in enumerate(step):
        if mask >> bit & 1:
            value = value + amount
    return value


def make_tables(owner, dp, mp):
    shape = (DPN * MPN, DPN * MPN)
    down = lax.broadcasted_iota(jnp.int32, shape, 0)
    along = lax.broadcasted_iota(jnp.int32, shape, 1)

    def pick(mask, value):
        return jnp.sum(jnp.where(mask, value, 0), axis=0, keepdims=True)

    across = jnp.broadcast_to(owner, shape)
    mine = jnp.sum(jnp.where(down == along, across, 0), axis=1, keepdims=True)
    mine = jnp.broadcast_to(mine, shape)
    before = ((down >> 4) == (along >> 4)) & (across < mine)
    rank = jnp.sum(jnp.where(before, 1, 0), axis=1, keepdims=True)
    rank = jnp.broadcast_to(rank, shape)
    column = down - dp * MPN
    in_band = (down >> 4) == dp
    sent = ((rank >> 1) ^ dp) * 2 + (rank & 1)
    met = ((down >> 4) ^ dp) * 2 + (rank & 1)
    slot_col = pick(in_band & (sent == along), column)
    hop_slot = pick(mine == dp * MPN + ((along & 15) ^ mp), met)
    slot_hop = pick(((mine >> 4) == dp) & (met == along), (mine & 15) ^ mp)
    col_slot = pick(in_band & (column == along), sent)
    flipped = (pick(mine == dp * MPN + mp, met) >> 1) & 1
    return slot_col, hop_slot, slot_hop, col_slot, flipped, 1 - flipped


def kernel(owners, grad, left, right, lroot, rroot, lst, rst, ob, *scratch):
    it = iter(scratch)

    def take(count):
        return [next(it) for _ in range(count)]

    gb = take(KR)
    s1, r1, s2, s3, r3, s4, r5 = (take(K) for _ in range(7))
    gq, lb, rb, la, pb = take(5)
    own_row, tab_rows, tab = take(3)
    sq_own, sq_in1, sq_mid, sq_in2 = take(4)
    ssem, rsem, qs, qr, gsem, wsem, tsem = take(7)

    dp = lax.axis_index("dp")
    mp = lax.axis_index("mp")
    dp_step, mp_step = steps(dp, 3), steps(mp, 4)
    dp_peer = [
        (xor(dp, i, dp_step), xor(mp, 8 * (i % 2), mp_step)) for i in range(DPN)
    ]
    mp_peer = [(dp, xor(mp, q, mp_step)) for q in range(MPN)]

    barrier = pltpu.get_barrier_semaphore()
    for peer in dp_peer[1:] + mp_peer[1:]:
        pl.semaphore_signal(barrier, inc=1, device_id=peer, device_id_type=MESH)

    load_owners = pltpu.make_async_copy(owners, own_row, tsem.at[0])
    load_owners.start()

    def load_grad(r):
        for n in range(MPN):
            here = (pl.ds(ROWT * r, ROWT), pl.ds(BLK * n, BLK))
            pltpu.make_async_copy(grad.at[here], gb[r].at[n], gsem.at[r]).start()

    load_grad(0)

    load_owners.wait()
    tab_rows[...] = jnp.zeros_like(tab_rows)
    for n, row in enumerate(make_tables(own_row[...], dp, mp)):
        tab_rows[pl.ds(n, 1), :] = row & 15
    load_tables = pltpu.make_async_copy(tab_rows, tab, tsem.at[1])
    load_tables.start()
    load_tables.wait()

    def send(src, dst, phase, k, peer):
        pltpu.make_async_remote_copy(
            src_ref=src,
            dst_ref=dst,
            send_sem=ssem.at[phase, k],
            recv_sem=rsem.at[phase, k],
            device_id=peer,
            device_id_type=MESH,
        ).start()

    def take_bytes(ref, sem):
        pltpu.make_async_copy(ref, ref, sem).wait()

    seen = set()

    def first_hop(k):
        r, c0, width = CHUNKS[k]
        if r not in seen:
            seen.add(r)
            take_bytes(gb[r], gsem.at[r])
        for i in list(range(1, DPN)) + [0]:
            for n in (2 * i, 2 * i + 1):
                piece = gb[r][tab[0, n], :, pl.ds(c0, width)]
                if i:
                    s1[k][n] = piece
                else:
                    r1[k][n] = piece
            if i:
                if k == 0 and i == 1:
                    pl.semaphore_wait(barrier, DPN - 1 + MPN - 1)
                pair = pl.ds(2 * i, 2)
                send(s1[k].at[pair], r1[k].at[pair], 0, k, dp_peer[i])

    half, low = lax.div(mp, 8), lax.rem(mp, 8)

    def second_hop(k):
        r, c0, width = CHUNKS[k]
        take_bytes(s1[k].at[pl.ds(2, MPN - 2)], rsem.at[0, k])
        for q in range(MPN - 1, -1, -1):
            piece = r1[k][tab[1, q]]
            here = gq.at[half, low, r, :, pl.ds(c0, width)]
            if q:
                s2[k][q] = piece
                send(s2[k].at[q], here, 1, k, mp_peer[q])
            else:
                gq[half, low, r, :, pl.ds(c0, width)] = piece

    def square_tile(r, acc):
        def body(n, acc):
            x = gb[r][n].astype(jnp.float32)
            x = x * x
            for w in range(BLK // 128):
                acc = acc + x[:8, w * 128 : (w + 1) * 128] + x[8:, w * 128 : (w + 1) * 128]
            return acc

        return lax.fori_loop(0, MPN, body, acc)

    def send_square(src, dst, stage, peer):
        pltpu.make_async_remote_copy(
            src_ref=src,
            dst_ref=dst,
            send_sem=qs.at[stage],
            recv_sem=qr.at[stage],
            device_id=peer,
            device_id_type=MESH,
        ).start()

    for k in range(min(AHEAD, K)):
        if k == 1:
            for r in range(1, KR):
                load_grad(r)
        first_hop(k)
    for r in range(KR):
        if r not in seen:
            seen.add(r)
            take_bytes(gb[r], gsem.at[r])
    loads = [
        pltpu.make_async_copy(lroot, lb, wsem.at[0]),
        pltpu.make_async_copy(rroot, rb, wsem.at[1]),
        pltpu.make_async_copy(left, lst, wsem.at[2]),
        pltpu.make_async_copy(right, rst, wsem.at[3]),
    ]
    for c in loads:
        c.start()
    acc = jnp.zeros((8, 128), jnp.float32)
    for r in range(KR):
        acc = square_tile(r, acc)
    sq_own[...] = acc
    for i in range(1, DPN):
        send_square(sq_own, sq_in1.at[i], 0, dp_peer[i])
    for k in range(K):
        second_hop(k)
        if k + AHEAD < K:
            first_hop(k + AHEAD)
        if k == 1:
            take_bytes(sq_in1.at[pl.ds(1, DPN - 1)], qr.at[0])
            mid = sq_own[...]
            for i in range(1, DPN):
                mid = mid + sq_in1[i]
            sq_mid[...] = mid
            for q in range(1, MPN):
                send_square(sq_mid, sq_in2.at[q], 1, mp_peer[q])
    for c in loads:
        c.wait()
    take_bytes(sq_in2.at[pl.ds(1, MPN - 1)], qr.at[1])
    total = sq_mid[...]
    for q in range(1, MPN):
        total = total + sq_in2[q]
    total = jnp.sum(jnp.sum(total, axis=0, keepdims=True), axis=1, keepdims=True)
    mean_square = total / (DPN * BLK * MPN * BLK)
    scale = clip_level / jnp.sqrt(mean_square + 1e-06)
    factor = (1.0 - beta_stat) * scale * scale / BLK
    for k in range(K):
        take_bytes(s2[k].at[pl.ds(1, MPN - 1)], rsem.at[1, k])

    side = [tab[4, 0], tab[5, 0]]
    rows = MPN * ROWT

    def third_hop(k):
        r, c0, width = CHUNKS[k]
        if c0 == 0:
            for h in range(2):
                la[pl.ds(h * rows // 2, rows // 2), :] = lb[side[h], :, r].reshape(
                    rows // 2, BLK
                )

            @pl.loop(0, BLK // TILE)
            def _(n):
                at = pl.ds(pl.multiple_of(n * TILE, TILE), TILE)
                out = jnp.dot(
                    la[:, : BLK // 2],
                    gq[side[0], :, :, :, at].reshape(BLK // 2, TILE),
                    preferred_element_type=jnp.float32,
                )
                out += jnp.dot(
                    la[:, BLK // 2 :],
                    gq[side[1], :, :, :, at].reshape(BLK // 2, TILE),
                    preferred_element_type=jnp.float32,
                )
                pb[:, at] = out.astype(jnp.bfloat16)

        for n in range(width // TILE):
            out = jnp.dot(
                pb[...],
                rb[:, pl.ds(c0 + n * TILE, TILE)],
                preferred_element_type=jnp.float32,
            )
            out = (out * scale).astype(jnp.bfloat16)
            s3[k][:, :, pl.ds(n * TILE, TILE)] = out.reshape(MPN, ROWT, TILE)
        for q in range(MPN - 1, 0, -1):
            send(s3[k].at[mp_peer[q][1]], r3[k].at[q], 2, k, mp_peer[q])
        r3[k][0] = s3[k][mp]

    def fourth_hop(k):
        take_bytes(s2[k].at[pl.ds(1, MPN - 1)], rsem.at[2, k])
        for i in list(range(1, DPN)) + [0]:
            for n in (2 * i, 2 * i + 1):
                piece = r3[k][tab[2, n]]
                if i:
                    s4[k][n] = piece
                else:
                    r5[k][n] = piece
            if i:
                pair = pl.ds(2 * i, 2)
                send(s4[k].at[pair], r5[k].at[pair], 3, k, dp_peer[i])

    def left_part(n):
        here = pl.ds(n * TILE, TILE)
        tiles = TILE // SHARD
        lhs = gq[side[n // 2], pl.ds((n % 2) * tiles, tiles)].reshape(TILE, BLK)
        for g in range(2):
            cols = pl.ds(g * BLK // 2, BLK // 2)
            gram = lax.dot_general(
                lhs,
                gq[side[g]].reshape(BLK // 2, BLK),
                (((1,), (1,)), ((), ())),
                preferred_element_type=jnp.float32,
            )
            lst[here, cols] = beta_stat * lst[here, cols] + factor * gram

    def right_part(n):
        here = pl.ds(n * TILE, TILE)
        gram = lax.dot_general(
            gq[:, :, :, :, here].reshape(BLK, TILE),
            gq[...].reshape(BLK, BLK),
            (((0,), (0,)), ((), ())),
            preferred_element_type=jnp.float32,
        )
        rst[here, :] = beta_stat * rst[here, :] + factor * gram

    parts = [functools.partial(left_part, n) for n in range(4)]
    parts += [functools.partial(right_part, n) for n in range(4)]

    for k in range(K + BEHIND):
        if k < K:
            third_hop(k)
        if k >= BEHIND:
            fourth_hop(k - BEHIND)
            if parts:
                parts.pop(0)()
    for part in parts:
        part()

    for k in range(K):
        r, c0, width = CHUNKS[k]
        take_bytes(s1[k].at[pl.ds(2, MPN - 2)], rsem.at[3, k])
        for col in range(MPN):
            here = pl.ds(col * BLK + c0, width)
            ob[pl.ds(r * ROWT, ROWT), here] = r5[k][tab[3, col]]

    for k in range(K):
        take_bytes(s1[k].at[pl.ds(2, MPN - 2)], ssem.at[0, k])
        take_bytes(s2[k].at[pl.ds(1, MPN - 1)], ssem.at[1, k])
        take_bytes(s2[k].at[pl.ds(1, MPN - 1)], ssem.at[2, k])
        take_bytes(s1[k].at[pl.ds(2, MPN - 2)], ssem.at[3, k])
    take_bytes(sq_in1.at[pl.ds(1, DPN - 1)], qs.at[0])
    take_bytes(sq_in2.at[pl.ds(1, MPN - 1)], qs.at[1])


def move(*refs):
    count = (len(refs) - 1) // 2
    copies = []
    for n in range(count):
        rows = refs[n].shape[0] // MOVES
        for part in range(MOVES):
            here = pl.ds(part * rows, rows)
            sem = refs[-1].at[n, part]
            copies.append(
                pltpu.make_async_copy(refs[n].at[here], refs[count + n].at[here], sem)
            )
    for c in copies:
        c.start()
    for c in copies:
        c.wait()


def per_device(grad, block_owner, left_stat, right_stat, left_root, right_root):
    bf, f32 = jnp.bfloat16, jnp.float32
    hbm = pl.BlockSpec(memory_space=pl.ANY)
    hops = [pltpu.VMEM((MPN, ROWT, width), bf) for _, _, width in CHUNKS]
    dma = pltpu.SemaphoreType.DMA
    vmem = pl.BlockSpec(memory_space=pltpu.VMEM)
    outs = (((BLK, BLK), f32), ((BLK, BLK), f32), (grad.shape, bf))
    done = pl.pallas_call(
        kernel,
        name="shampoo",
        out_shape=tuple(pltpu.VMEM(*o) for o in outs),
        in_specs=[pl.BlockSpec(memory_space=pltpu.HBM)] * 6,
        out_specs=(vmem, vmem, vmem),
        scratch_shapes=[pltpu.VMEM((MPN, ROWT, BLK), bf) for _ in range(KR)]
        + hops * 7
        + [
            pltpu.VMEM((2, 8, KR, ROWT, BLK), bf),
            pltpu.VMEM((2, 8, KR, ROWT, BLK), bf),
            pltpu.VMEM((BLK, BLK), bf),
            pltpu.VMEM((MPN * ROWT, BLK), bf),
            pltpu.VMEM((MPN * ROWT, BLK), bf),
            pltpu.VMEM((1, DPN * MPN), jnp.int32),
            pltpu.VMEM((8, DPN * MPN), jnp.int32),
            pltpu.SMEM((8, DPN * MPN), jnp.int32),
            pltpu.VMEM((8, 128), f32),
            pltpu.VMEM((DPN, 8, 128), f32),
            pltpu.VMEM((8, 128), f32),
            pltpu.VMEM((MPN, 8, 128), f32),
            dma((4, K)),
            dma((4, K)),
            dma((2,)),
            dma((2,)),
            dma((KR,)),
            dma((4,)),
            dma((2,)),
        ],
        compiler_params=pltpu.CompilerParams(
            collective_id=0, has_side_effects=True, vmem_limit_bytes=44 << 20
        ),
    )(
        block_owner.reshape(1, DPN * MPN),
        grad,
        left_stat[0],
        right_stat[0],
        left_root[0].reshape(2, 8, KR, ROWT, BLK),
        right_root[0],
    )
    new_left, new_right, update = pl.pallas_call(
        move,
        name="move",
        out_shape=tuple(jax.ShapeDtypeStruct(*o) for o in outs),
        in_specs=(vmem,) * 3,
        out_specs=(hbm,) * 3,
        scratch_shapes=[dma((3, MOVES))],
        compiler_params=pltpu.CompilerParams(vmem_limit_bytes=1 << 20),
    )(*(pltpu.with_memory_space_constraint(d, pltpu.VMEM) for d in done))
    return (new_left[None], new_right[None], update)


def solution(mesh):
    both = ("dp", "mp")
    in_specs = (
        P(both, None),
        P(),
        P(both, None, None),
        P(both, None, None),
        P(both, None, None),
        P(both, None, None),
    )
    out_specs = (P(both, None, None), P(both, None, None), P(both, None))
    return jax.shard_map(
        per_device, mesh=mesh, in_specs=in_specs, out_specs=out_specs, check_vma=False
    )
```

```python
import functools

import jax
import jax.numpy as jnp
from jax import lax
from jax.experimental import pallas as pl
from jax.experimental.pallas import tpu as pltpu
from jax.sharding import PartitionSpec as P

MESH = pl.DeviceIdType.MESH
BLK = 1024
DPN = 8
MPN = 16
SHARD = 64
ROWT = 16
KR = SHARD // ROWT
CHUNKS = [(row, col, 512) for row in range(4) for col in (0, 512)]
K = len(CHUNKS)
AHEAD = 3
BEHIND = 3
TILE = 256
ORDER1 = (1, 2, 3, 4, 5, 6, 7, 0)
ORDER2 = tuple(range(15, -1, -1))
ORDER3 = tuple(range(15, 0, -1))
ORDER4 = (7, 6, 5, 4, 3, 2, 1, 0)
SUM_AT = -1
LOAD_AT = (-1, -1, -1, -1)
MOVES = 4

clip_level = 0.5
beta_stat = 0.95


def steps(value, bits):
    return [
        (1 << bit) * (1 - 2 * lax.rem(lax.div(value, 1 << bit), 2)) for bit in range(bits)
    ]


def xor(value, mask, step):
    for bit, amount in enumerate(step):
        if mask >> bit & 1:
            value = value + amount
    return value


def make_tables(owner, dp, mp):
    shape = (DPN * MPN, DPN * MPN)
    down = lax.broadcasted_iota(jnp.int32, shape, 0)
    along = lax.broadcasted_iota(jnp.int32, shape, 1)

    def pick(mask, value):
        return jnp.sum(jnp.where(mask, value, 0), axis=0, keepdims=True)

    across = jnp.broadcast_to(owner, shape)
    mine = jnp.sum(jnp.where(down == along, across, 0), axis=1, keepdims=True)
    mine = jnp.broadcast_to(mine, shape)
    before = ((down >> 4) == (along >> 4)) & (across < mine)
    rank = jnp.sum(jnp.where(before, 1, 0), axis=1, keepdims=True)
    rank = jnp.broadcast_to(rank, shape)
    column = down - dp * MPN
    in_band = (down >> 4) == dp
    sent = ((rank >> 1) ^ dp) * 2 + (rank & 1)
    met = ((down >> 4) ^ dp) * 2 + (rank & 1)
    slot_col = pick(in_band & (sent == along), column)
    hop_slot = pick(mine == dp * MPN + ((along & 15) ^ mp), met)
    slot_hop = pick(((mine >> 4) == dp) & (met == along), (mine & 15) ^ mp)
    col_slot = pick(in_band & (column == along), sent)
    flipped = (pick(mine == dp * MPN + mp, met) >> 1) & 1
    return slot_col, hop_slot, slot_hop, col_slot, flipped, 1 - flipped


def kernel(owners, grad, left, right, lroot, rroot, lst, rst, ob, *scratch):
    it = iter(scratch)

    def take(count):
        return [next(it) for _ in range(count)]

    gb = take(KR)
    s1, r1, s2, s3, r3, s4, r5 = (take(K) for _ in range(7))
    gq, lb, rb, la, pb = take(5)
    own_row, tab_rows, tab = take(3)
    sq_own, sq_in1, sq_mid, sq_in2 = take(4)
    ssem, rsem, qs, qr, gsem, wsem, tsem = take(7)

    dp = lax.axis_index("dp")
    mp = lax.axis_index("mp")
    dp_step, mp_step = steps(dp, 3), steps(mp, 4)
    dp_peer = [
        (xor(dp, i, dp_step), xor(mp, 8 * (i % 2), mp_step)) for i in range(DPN)
    ]
    mp_peer = [(dp, xor(mp, q, mp_step)) for q in range(MPN)]

    barrier = pltpu.get_barrier_semaphore()
    for peer in dp_peer[1:] + mp_peer[1:]:
        pl.semaphore_signal(barrier, inc=1, device_id=peer, device_id_type=MESH)

    load_owners = pltpu.make_async_copy(owners, own_row, tsem.at[0])
    load_owners.start()

    def load_grad(r):
        for n in range(MPN):
            here = (pl.ds(ROWT * r, ROWT), pl.ds(BLK * n, BLK))
            pltpu.make_async_copy(grad.at[here], gb[r].at[n], gsem.at[r]).start()

    load_grad(0)

    load_owners.wait()
    tab_rows[...] = jnp.zeros_like(tab_rows)
    for n, row in enumerate(make_tables(own_row[...], dp, mp)):
        tab_rows[pl.ds(n, 1), :] = row & 15
    load_tables = pltpu.make_async_copy(tab_rows, tab, tsem.at[1])
    load_tables.start()
    load_tables.wait()

    def send(src, dst, phase, k, peer):
        pltpu.make_async_remote_copy(
            src_ref=src,
            dst_ref=dst,
            send_sem=ssem.at[phase, k],
            recv_sem=rsem.at[phase, k],
            device_id=peer,
            device_id_type=MESH,
        ).start()

    def take_bytes(ref, sem):
        pltpu.make_async_copy(ref, ref, sem).wait()

    seen = set()

    def first_hop(k):
        r, c0, width = CHUNKS[k]
        if r not in seen:
            seen.add(r)
            take_bytes(gb[r], gsem.at[r])
        for i in ORDER1:
            for n in (2 * i, 2 * i + 1):
                piece = gb[r][tab[0, n], :, pl.ds(c0, width)]
                if i:
                    s1[k][n] = piece
                else:
                    r1[k][n] = piece
            if i:
                if k == 0 and i == ORDER1[0]:
                    pl.semaphore_wait(barrier, DPN - 1 + MPN - 1)
                pair = pl.ds(2 * i, 2)
                send(s1[k].at[pair], r1[k].at[pair], 0, k, dp_peer[i])

    half, low = lax.div(mp, 8), lax.rem(mp, 8)

    def second_hop(k):
        r, c0, width = CHUNKS[k]
        take_bytes(s1[k].at[pl.ds(2, MPN - 2)], rsem.at[0, k])
        for q in ORDER2:
            piece = r1[k][tab[1, q]]
            here = gq.at[half, low, r, :, pl.ds(c0, width)]
            if q:
                s2[k][q] = piece
                send(s2[k].at[q], here, 1, k, mp_peer[q])
            else:
                gq[half, low, r, :, pl.ds(c0, width)] = piece

    def square_tile(r, acc):
        def body(n, acc):
            x = gb[r][n].astype(jnp.float32)
            x = x * x
            for w in range(BLK // 128):
                acc = acc + x[:8, w * 128 : (w + 1) * 128] + x[8:, w * 128 : (w + 1) * 128]
            return acc

        return lax.fori_loop(0, MPN, body, acc)

    def send_square(src, dst, stage, peer):
        pltpu.make_async_remote_copy(
            src_ref=src,
            dst_ref=dst,
            send_sem=qs.at[stage],
            recv_sem=qr.at[stage],
            device_id=peer,
            device_id_type=MESH,
        ).start()

    for k in range(min(AHEAD, K)):
        if k == 1:
            for r in range(1, KR):
                load_grad(r)
        first_hop(k)
    loads = [
        pltpu.make_async_copy(lroot, lb, wsem.at[0]),
        pltpu.make_async_copy(rroot, rb, wsem.at[1]),
        pltpu.make_async_copy(left, lst, wsem.at[2]),
        pltpu.make_async_copy(right, rst, wsem.at[3]),
    ]

    def squares():
        for r in range(KR):
            if r not in seen:
                seen.add(r)
                take_bytes(gb[r], gsem.at[r])
        acc = jnp.zeros((8, 128), jnp.float32)
        for r in range(KR):
            acc = square_tile(r, acc)
        sq_own[...] = acc
        for i in range(1, DPN):
            send_square(sq_own, sq_in1.at[i], 0, dp_peer[i])

    for k in range(-1, K):
        if k >= 0:
            second_hop(k)
            if k + AHEAD < K:
                first_hop(k + AHEAD)
        if k == SUM_AT:
            squares()
        for n in range(4):
            if k == LOAD_AT[n]:
                loads[n].start()
        if k == SUM_AT + 2:
            take_bytes(sq_in1.at[pl.ds(1, DPN - 1)], qr.at[0])
            mid = sq_own[...]
            for i in range(1, DPN):
                mid = mid + sq_in1[i]
            sq_mid[...] = mid
            for q in range(1, MPN):
                send_square(sq_mid, sq_in2.at[q], 1, mp_peer[q])
    for c in loads:
        c.wait()
    take_bytes(sq_in2.at[pl.ds(1, MPN - 1)], qr.at[1])
    total = sq_mid[...]
    for q in range(1, MPN):
        total = total + sq_in2[q]
    total = jnp.sum(jnp.sum(total, axis=0, keepdims=True), axis=1, keepdims=True)
    mean_square = total / (DPN * BLK * MPN * BLK)
    scale = clip_level / jnp.sqrt(mean_square + 1e-06)
    factor = (1.0 - beta_stat) * scale * scale / BLK
    for k in range(K):
        take_bytes(s2[k].at[pl.ds(1, MPN - 1)], rsem.at[1, k])

    side = [tab[4, 0], tab[5, 0]]
    rows = MPN * ROWT

    def third_hop(k):
        r, c0, width = CHUNKS[k]
        if c0 == 0:
            for h in range(2):
                la[pl.ds(h * rows // 2, rows // 2), :] = lb[side[h], :, r].reshape(
                    rows // 2, BLK
                )

            @pl.loop(0, BLK // TILE)
            def _(n):
                at = pl.ds(pl.multiple_of(n * TILE, TILE), TILE)
                out = jnp.dot(
                    la[:, : BLK // 2],
                    gq[side[0], :, :, :, at].reshape(BLK // 2, TILE),
                    preferred_element_type=jnp.float32,
                )
                out += jnp.dot(
                    la[:, BLK // 2 :],
                    gq[side[1], :, :, :, at].reshape(BLK // 2, TILE),
                    preferred_element_type=jnp.float32,
                )
                pb[:, at] = out.astype(jnp.bfloat16)

        for n in range(width // TILE):
            out = jnp.dot(
                pb[...],
                rb[:, pl.ds(c0 + n * TILE, TILE)],
                preferred_element_type=jnp.float32,
            )
            out = (out * scale).astype(jnp.bfloat16)
            s3[k][:, :, pl.ds(n * TILE, TILE)] = out.reshape(MPN, ROWT, TILE)
        for q in ORDER3:
            send(s3[k].at[mp_peer[q][1]], r3[k].at[q], 2, k, mp_peer[q])
        r3[k][0] = s3[k][mp]

    def fourth_hop(k):
        take_bytes(s2[k].at[pl.ds(1, MPN - 1)], rsem.at[2, k])
        for i in ORDER4:
            for n in (2 * i, 2 * i + 1):
                piece = r3[k][tab[2, n]]
                if i:
                    s4[k][n] = piece
                else:
                    r5[k][n] = piece
            if i:
                pair = pl.ds(2 * i, 2)
                send(s4[k].at[pair], r5[k].at[pair], 3, k, dp_peer[i])

    def left_part(n):
        here = pl.ds(n * TILE, TILE)
        tiles = TILE // SHARD
        lhs = gq[side[n // 2], pl.ds((n % 2) * tiles, tiles)].reshape(TILE, BLK)
        for g in range(2):
            cols = pl.ds(g * BLK // 2, BLK // 2)
            gram = lax.dot_general(
                lhs,
                gq[side[g]].reshape(BLK // 2, BLK),
                (((1,), (1,)), ((), ())),
                preferred_element_type=jnp.float32,
            )
            lst[here, cols] = beta_stat * lst[here, cols] + factor * gram

    def right_part(n):
        here = pl.ds(n * TILE, TILE)
        gram = lax.dot_general(
            gq[:, :, :, :, here].reshape(BLK, TILE),
            gq[...].reshape(BLK, BLK),
            (((0,), (0,)), ((), ())),
            preferred_element_type=jnp.float32,
        )
        rst[here, :] = beta_stat * rst[here, :] + factor * gram

    parts = [functools.partial(left_part, n) for n in range(4)]
    parts += [functools.partial(right_part, n) for n in range(4)]

    for k in range(K + BEHIND):
        if k < K:
            third_hop(k)
        if k >= BEHIND:
            fourth_hop(k - BEHIND)
            if parts:
                parts.pop(0)()
    for part in parts:
        part()

    for k in range(K):
        r, c0, width = CHUNKS[k]
        take_bytes(s1[k].at[pl.ds(2, MPN - 2)], rsem.at[3, k])
        for col in range(MPN):
            here = pl.ds(col * BLK + c0, width)
            ob[pl.ds(r * ROWT, ROWT), here] = r5[k][tab[3, col]]

    for k in range(K):
        take_bytes(s1[k].at[pl.ds(2, MPN - 2)], ssem.at[0, k])
        take_bytes(s2[k].at[pl.ds(1, MPN - 1)], ssem.at[1, k])
        take_bytes(s2[k].at[pl.ds(1, MPN - 1)], ssem.at[2, k])
        take_bytes(s1[k].at[pl.ds(2, MPN - 2)], ssem.at[3, k])
    take_bytes(sq_in1.at[pl.ds(1, DPN - 1)], qs.at[0])
    take_bytes(sq_in2.at[pl.ds(1, MPN - 1)], qs.at[1])


def move(*refs):
    count = (len(refs) - 1) // 2
    copies = []
    for n in range(count):
        rows = refs[n].shape[0] // MOVES
        for part in range(MOVES):
            here = pl.ds(part * rows, rows)
            sem = refs[-1].at[n, part]
            copies.append(
                pltpu.make_async_copy(refs[n].at[here], refs[count + n].at[here], sem)
            )
    for c in copies:
        c.start()
    for c in copies:
        c.wait()


def per_device(grad, block_owner, left_stat, right_stat, left_root, right_root):
    bf, f32 = jnp.bfloat16, jnp.float32
    hbm = pl.BlockSpec(memory_space=pl.ANY)
    hops = [pltpu.VMEM((MPN, ROWT, width), bf) for _, _, width in CHUNKS]
    dma = pltpu.SemaphoreType.DMA
    vmem = pl.BlockSpec(memory_space=pltpu.VMEM)
    outs = (((BLK, BLK), f32), ((BLK, BLK), f32), (grad.shape, bf))
    done = pl.pallas_call(
        kernel,
        name="shampoo",
        out_shape=tuple(pltpu.VMEM(*o) for o in outs),
        in_specs=[pl.BlockSpec(memory_space=pltpu.HBM)] * 6,
        out_specs=(vmem, vmem, vmem),
        scratch_shapes=[pltpu.VMEM((MPN, ROWT, BLK), bf) for _ in range(KR)]
        + hops * 7
        + [
            pltpu.VMEM((2, 8, KR, ROWT, BLK), bf),
            pltpu.VMEM((2, 8, KR, ROWT, BLK), bf),
            pltpu.VMEM((BLK, BLK), bf),
            pltpu.VMEM((MPN * ROWT, BLK), bf),
            pltpu.VMEM((MPN * ROWT, BLK), bf),
            pltpu.VMEM((1, DPN * MPN), jnp.int32),
            pltpu.VMEM((8, DPN * MPN), jnp.int32),
            pltpu.SMEM((8, DPN * MPN), jnp.int32),
            pltpu.VMEM((8, 128), f32),
            pltpu.VMEM((DPN, 8, 128), f32),
            pltpu.VMEM((8, 128), f32),
            pltpu.VMEM((MPN, 8, 128), f32),
            dma((4, K)),
            dma((4, K)),
            dma((2,)),
            dma((2,)),
            dma((KR,)),
            dma((4,)),
            dma((2,)),
        ],
        compiler_params=pltpu.CompilerParams(
            collective_id=0, has_side_effects=True, vmem_limit_bytes=44 << 20
        ),
    )(
        block_owner.reshape(1, DPN * MPN),
        grad,
        left_stat[0],
        right_stat[0],
        left_root[0].reshape(2, 8, KR, ROWT, BLK),
        right_root[0],
    )
    new_left, new_right, update = pl.pallas_call(
        move,
        name="move",
        out_shape=tuple(jax.ShapeDtypeStruct(*o) for o in outs),
        in_specs=(vmem,) * 3,
        out_specs=(hbm,) * 3,
        scratch_shapes=[dma((3, MOVES))],
        compiler_params=pltpu.CompilerParams(vmem_limit_bytes=1 << 20),
    )(*(pltpu.with_memory_space_constraint(d, pltpu.VMEM) for d in done))
    return (new_left[None], new_right[None], update)


def solution(mesh):
    both = ("dp", "mp")
    in_specs = (
        P(both, None),
        P(),
        P(both, None, None),
        P(both, None, None),
        P(both, None, None),
        P(both, None, None),
    )
    out_specs = (P(both, None, None), P(both, None, None), P(both, None))
    return jax.shard_map(
        per_device, mesh=mesh, in_specs=in_specs, out_specs=out_specs, check_vma=False
    )
```

```python
import functools

import jax
import jax.numpy as jnp
from jax import lax
from jax.experimental import pallas as pl
from jax.experimental.pallas import tpu as pltpu
from jax.sharding import PartitionSpec as P

MESH = pl.DeviceIdType.MESH
BLK = 1024
DPN = 8
MPN = 16
SHARD = 64
ROWT = 16
KR = SHARD // ROWT
CHUNKS = [(row, col, 512) for row in range(4) for col in (0, 512)]
K = len(CHUNKS)
WINDOW = ((0, 1), (2, 3), (4, 5), (6,), (7,))
BEHIND = 3
TILE = 256
ORDER1 = (1, 2, 3, 4, 5, 6, 7, 0)
ORDER2 = tuple(range(15, -1, -1))
ORDER3 = tuple(range(15, 0, -1))
ORDER4 = (7, 6, 5, 4, 3, 2, 1, 0)
SUM_AT = -1
LOAD_AT = (-1, -1, -1, -1)
MOVES = 4

clip_level = 0.5
beta_stat = 0.95


def steps(value, bits):
    return [
        (1 << bit) * (1 - 2 * lax.rem(lax.div(value, 1 << bit), 2)) for bit in range(bits)
    ]


def xor(value, mask, step):
    for bit, amount in enumerate(step):
        if mask >> bit & 1:
            value = value + amount
    return value


def make_tables(owner, dp, mp):
    shape = (DPN * MPN, DPN * MPN)
    down = lax.broadcasted_iota(jnp.int32, shape, 0)
    along = lax.broadcasted_iota(jnp.int32, shape, 1)

    def pick(mask, value):
        return jnp.sum(jnp.where(mask, value, 0), axis=0, keepdims=True)

    across = jnp.broadcast_to(owner, shape)
    mine = jnp.sum(jnp.where(down == along, across, 0), axis=1, keepdims=True)
    mine = jnp.broadcast_to(mine, shape)
    before = ((down >> 4) == (along >> 4)) & (across < mine)
    rank = jnp.sum(jnp.where(before, 1, 0), axis=1, keepdims=True)
    rank = jnp.broadcast_to(rank, shape)
    column = down - dp * MPN
    in_band = (down >> 4) == dp
    sent = ((rank >> 1) ^ dp) * 2 + (rank & 1)
    met = ((down >> 4) ^ dp) * 2 + (rank & 1)
    slot_col = pick(in_band & (sent == along), column)
    hop_slot = pick(mine == dp * MPN + ((along & 15) ^ mp), met)
    slot_hop = pick(((mine >> 4) == dp) & (met == along), (mine & 15) ^ mp)
    col_slot = pick(in_band & (column == along), sent)
    flipped = (pick(mine == dp * MPN + mp, met) >> 1) & 1
    return slot_col, hop_slot, slot_hop, col_slot, flipped, 1 - flipped


def kernel(owners, grad, left, right, lroot, rroot, lst, rst, ob, *scratch):
    it = iter(scratch)

    def take(count):
        return [next(it) for _ in range(count)]

    gb = take(KR)
    s1, r1, s2, s3, r3, s4, r5 = (take(K) for _ in range(7))
    gq, lb, rb, la, pb = take(5)
    own_row, tab_rows, tab = take(3)
    sq_own, sq_in1, sq_mid, sq_in2 = take(4)
    ssem, rsem, qs, qr, gsem, wsem, tsem = take(7)

    dp = lax.axis_index("dp")
    mp = lax.axis_index("mp")
    dp_step, mp_step = steps(dp, 3), steps(mp, 4)
    dp_peer = [
        (xor(dp, i, dp_step), xor(mp, 8 * (i % 2), mp_step)) for i in range(DPN)
    ]
    mp_peer = [(dp, xor(mp, q, mp_step)) for q in range(MPN)]

    barrier = pltpu.get_barrier_semaphore()
    for peer in dp_peer[1:] + mp_peer[1:]:
        pl.semaphore_signal(barrier, inc=1, device_id=peer, device_id_type=MESH)

    load_owners = pltpu.make_async_copy(owners, own_row, tsem.at[0])
    load_owners.start()

    def load_grad(r):
        for n in range(MPN):
            here = (pl.ds(ROWT * r, ROWT), pl.ds(BLK * n, BLK))
            pltpu.make_async_copy(grad.at[here], gb[r].at[n], gsem.at[r]).start()

    load_grad(0)

    load_owners.wait()
    tab_rows[...] = jnp.zeros_like(tab_rows)
    for n, row in enumerate(make_tables(own_row[...], dp, mp)):
        tab_rows[pl.ds(n, 1), :] = row & 15
    load_tables = pltpu.make_async_copy(tab_rows, tab, tsem.at[1])
    load_tables.start()
    load_tables.wait()

    def send(src, dst, phase, k, peer):
        pltpu.make_async_remote_copy(
            src_ref=src,
            dst_ref=dst,
            send_sem=ssem.at[phase, k],
            recv_sem=rsem.at[phase, k],
            device_id=peer,
            device_id_type=MESH,
        ).start()

    def take_bytes(ref, sem):
        pltpu.make_async_copy(ref, ref, sem).wait()

    seen = set()

    def first_hop(k):
        r, c0, width = CHUNKS[k]
        if r not in seen:
            seen.add(r)
            take_bytes(gb[r], gsem.at[r])
        for i in ORDER1:
            for n in (2 * i, 2 * i + 1):
                piece = gb[r][tab[0, n], :, pl.ds(c0, width)]
                if i:
                    s1[k][n] = piece
                else:
                    r1[k][n] = piece
            if i:
                if k == 0 and i == ORDER1[0]:
                    pl.semaphore_wait(barrier, DPN - 1 + MPN - 1)
                pair = pl.ds(2 * i, 2)
                send(s1[k].at[pair], r1[k].at[pair], 0, k, dp_peer[i])

    half, low = lax.div(mp, 8), lax.rem(mp, 8)

    def second_hop(k):
        r, c0, width = CHUNKS[k]
        take_bytes(s1[k].at[pl.ds(2, MPN - 2)], rsem.at[0, k])
        for q in ORDER2:
            piece = r1[k][tab[1, q]]
            here = gq.at[half, low, r, :, pl.ds(c0, width)]
            if q:
                s2[k][q] = piece
                send(s2[k].at[q], here, 1, k, mp_peer[q])
            else:
                gq[half, low, r, :, pl.ds(c0, width)] = piece

    def square_tile(r, acc):
        def body(n, acc):
            x = gb[r][n].astype(jnp.float32)
            x = x * x
            for w in range(BLK // 128):
                acc = acc + x[:8, w * 128 : (w + 1) * 128] + x[8:, w * 128 : (w + 1) * 128]
            return acc

        return lax.fori_loop(0, MPN, body, acc)

    def send_square(src, dst, stage, peer):
        pltpu.make_async_remote_copy(
            src_ref=src,
            dst_ref=dst,
            send_sem=qs.at[stage],
            recv_sem=qr.at[stage],
            device_id=peer,
            device_id_type=MESH,
        ).start()

    for k in WINDOW[0]:
        if k == 1:
            for r in range(1, KR):
                load_grad(r)
        first_hop(k)
    loads = [
        pltpu.make_async_copy(lroot, lb, wsem.at[0]),
        pltpu.make_async_copy(rroot, rb, wsem.at[1]),
        pltpu.make_async_copy(left, lst, wsem.at[2]),
        pltpu.make_async_copy(right, rst, wsem.at[3]),
    ]

    def squares():
        for r in range(KR):
            if r not in seen:
                seen.add(r)
                take_bytes(gb[r], gsem.at[r])
        acc = jnp.zeros((8, 128), jnp.float32)
        for r in range(KR):
            acc = square_tile(r, acc)
        sq_own[...] = acc
        for i in range(1, DPN):
            send_square(sq_own, sq_in1.at[i], 0, dp_peer[i])

    for k in range(-1, K):
        if k >= 0:
            second_hop(k)
            for later in WINDOW[k + 1] if k + 1 < len(WINDOW) else ():
                first_hop(later)
        if k == SUM_AT:
            squares()
        for n in range(4):
            if k == LOAD_AT[n]:
                loads[n].start()
        if k == SUM_AT + 2:
            take_bytes(sq_in1.at[pl.ds(1, DPN - 1)], qr.at[0])
            mid = sq_own[...]
            for i in range(1, DPN):
                mid = mid + sq_in1[i]
            sq_mid[...] = mid
            for q in range(1, MPN):
                send_square(sq_mid, sq_in2.at[q], 1, mp_peer[q])
    for c in loads:
        c.wait()
    take_bytes(sq_in2.at[pl.ds(1, MPN - 1)], qr.at[1])
    total = sq_mid[...]
    for q in range(1, MPN):
        total = total + sq_in2[q]
    total = jnp.sum(jnp.sum(total, axis=0, keepdims=True), axis=1, keepdims=True)
    mean_square = total / (DPN * BLK * MPN * BLK)
    scale = clip_level / jnp.sqrt(mean_square + 1e-06)
    factor = (1.0 - beta_stat) * scale * scale / BLK
    for k in range(K):
        take_bytes(s2[k].at[pl.ds(1, MPN - 1)], rsem.at[1, k])

    side = [tab[4, 0], tab[5, 0]]
    rows = MPN * ROWT

    def third_hop(k):
        r, c0, width = CHUNKS[k]
        if c0 == 0:
            for h in range(2):
                la[pl.ds(h * rows // 2, rows // 2), :] = lb[side[h], :, r].reshape(
                    rows // 2, BLK
                )

            @pl.loop(0, BLK // TILE)
            def _(n):
                at = pl.ds(pl.multiple_of(n * TILE, TILE), TILE)
                out = jnp.dot(
                    la[:, : BLK // 2],
                    gq[side[0], :, :, :, at].reshape(BLK // 2, TILE),
                    preferred_element_type=jnp.float32,
                )
                out += jnp.dot(
                    la[:, BLK // 2 :],
                    gq[side[1], :, :, :, at].reshape(BLK // 2, TILE),
                    preferred_element_type=jnp.float32,
                )
                pb[:, at] = out.astype(jnp.bfloat16)

        for n in range(width // TILE):
            out = jnp.dot(
                pb[...],
                rb[:, pl.ds(c0 + n * TILE, TILE)],
                preferred_element_type=jnp.float32,
            )
            out = (out * scale).astype(jnp.bfloat16)
            s3[k][:, :, pl.ds(n * TILE, TILE)] = out.reshape(MPN, ROWT, TILE)
        for q in ORDER3:
            send(s3[k].at[mp_peer[q][1]], r3[k].at[q], 2, k, mp_peer[q])
        r3[k][0] = s3[k][mp]

    def fourth_hop(k):
        take_bytes(s2[k].at[pl.ds(1, MPN - 1)], rsem.at[2, k])
        for i in ORDER4:
            for n in (2 * i, 2 * i + 1):
                piece = r3[k][tab[2, n]]
                if i:
                    s4[k][n] = piece
                else:
                    r5[k][n] = piece
            if i:
                pair = pl.ds(2 * i, 2)
                send(s4[k].at[pair], r5[k].at[pair], 3, k, dp_peer[i])

    def left_part(n):
        here = pl.ds(n * TILE, TILE)
        tiles = TILE // SHARD
        lhs = gq[side[n // 2], pl.ds((n % 2) * tiles, tiles)].reshape(TILE, BLK)
        for g in range(2):
            cols = pl.ds(g * BLK // 2, BLK // 2)
            gram = lax.dot_general(
                lhs,
                gq[side[g]].reshape(BLK // 2, BLK),
                (((1,), (1,)), ((), ())),
                preferred_element_type=jnp.float32,
            )
            lst[here, cols] = beta_stat * lst[here, cols] + factor * gram

    def right_part(n):
        here = pl.ds(n * TILE, TILE)
        gram = lax.dot_general(
            gq[:, :, :, :, here].reshape(BLK, TILE),
            gq[...].reshape(BLK, BLK),
            (((0,), (0,)), ((), ())),
            preferred_element_type=jnp.float32,
        )
        rst[here, :] = beta_stat * rst[here, :] + factor * gram

    parts = [functools.partial(left_part, n) for n in range(4)]
    parts += [functools.partial(right_part, n) for n in range(4)]

    for k in range(K + BEHIND):
        if k < K:
            third_hop(k)
        if k >= BEHIND:
            fourth_hop(k - BEHIND)
            if parts:
                parts.pop(0)()
    for part in parts:
        part()

    for k in range(K):
        r, c0, width = CHUNKS[k]
        take_bytes(s1[k].at[pl.ds(2, MPN - 2)], rsem.at[3, k])
        for col in range(MPN):
            here = pl.ds(col * BLK + c0, width)
            ob[pl.ds(r * ROWT, ROWT), here] = r5[k][tab[3, col]]

    for k in range(K):
        take_bytes(s1[k].at[pl.ds(2, MPN - 2)], ssem.at[0, k])
        take_bytes(s2[k].at[pl.ds(1, MPN - 1)], ssem.at[1, k])
        take_bytes(s2[k].at[pl.ds(1, MPN - 1)], ssem.at[2, k])
        take_bytes(s1[k].at[pl.ds(2, MPN - 2)], ssem.at[3, k])
    take_bytes(sq_in1.at[pl.ds(1, DPN - 1)], qs.at[0])
    take_bytes(sq_in2.at[pl.ds(1, MPN - 1)], qs.at[1])


def move(*refs):
    count = (len(refs) - 1) // 2
    copies = []
    for n in range(count):
        rows = refs[n].shape[0] // MOVES
        for part in range(MOVES):
            here = pl.ds(part * rows, rows)
            sem = refs[-1].at[n, part]
            copies.append(
                pltpu.make_async_copy(refs[n].at[here], refs[count + n].at[here], sem)
            )
    for c in copies:
        c.start()
    for c in copies:
        c.wait()


def per_device(grad, block_owner, left_stat, right_stat, left_root, right_root):
    bf, f32 = jnp.bfloat16, jnp.float32
    hbm = pl.BlockSpec(memory_space=pl.ANY)
    hops = [pltpu.VMEM((MPN, ROWT, width), bf) for _, _, width in CHUNKS]
    dma = pltpu.SemaphoreType.DMA
    vmem = pl.BlockSpec(memory_space=pltpu.VMEM)
    outs = (((BLK, BLK), f32), ((BLK, BLK), f32), (grad.shape, bf))
    done = pl.pallas_call(
        kernel,
        name="shampoo",
        out_shape=tuple(pltpu.VMEM(*o) for o in outs),
        in_specs=[pl.BlockSpec(memory_space=pltpu.HBM)] * 6,
        out_specs=(vmem, vmem, vmem),
        scratch_shapes=[pltpu.VMEM((MPN, ROWT, BLK), bf) for _ in range(KR)]
        + hops * 7
        + [
            pltpu.VMEM((2, 8, KR, ROWT, BLK), bf),
            pltpu.VMEM((2, 8, KR, ROWT, BLK), bf),
            pltpu.VMEM((BLK, BLK), bf),
            pltpu.VMEM((MPN * ROWT, BLK), bf),
            pltpu.VMEM((MPN * ROWT, BLK), bf),
            pltpu.VMEM((1, DPN * MPN), jnp.int32),
            pltpu.VMEM((8, DPN * MPN), jnp.int32),
            pltpu.SMEM((8, DPN * MPN), jnp.int32),
            pltpu.VMEM((8, 128), f32),
            pltpu.VMEM((DPN, 8, 128), f32),
            pltpu.VMEM((8, 128), f32),
            pltpu.VMEM((MPN, 8, 128), f32),
            dma((4, K)),
            dma((4, K)),
            dma((2,)),
            dma((2,)),
            dma((KR,)),
            dma((4,)),
            dma((2,)),
        ],
        compiler_params=pltpu.CompilerParams(
            collective_id=0, has_side_effects=True, vmem_limit_bytes=44 << 20
        ),
    )(
        block_owner.reshape(1, DPN * MPN),
        grad,
        left_stat[0],
        right_stat[0],
        left_root[0].reshape(2, 8, KR, ROWT, BLK),
        right_root[0],
    )
    new_left, new_right, update = pl.pallas_call(
        move,
        name="move",
        out_shape=tuple(jax.ShapeDtypeStruct(*o) for o in outs),
        in_specs=(vmem,) * 3,
        out_specs=(hbm,) * 3,
        scratch_shapes=[dma((3, MOVES))],
        compiler_params=pltpu.CompilerParams(vmem_limit_bytes=1 << 20),
    )(*(pltpu.with_memory_space_constraint(d, pltpu.VMEM) for d in done))
    return (new_left[None], new_right[None], update)


def solution(mesh):
    both = ("dp", "mp")
    in_specs = (
        P(both, None),
        P(),
        P(both, None, None),
        P(both, None, None),
        P(both, None, None),
        P(both, None, None),
    )
    out_specs = (P(both, None, None), P(both, None, None), P(both, None))
    return jax.shard_map(
        per_device, mesh=mesh, in_specs=in_specs, out_specs=out_specs, check_vma=False
    )
```
